32 devices in a mesh: rep: 8 (over y, x, core), shard: 4 (over z).
Axes of the slice: x: 2, y: 2, z: 4, core: 2. Of those that a mesh axis runs over, the one named last changes fastest.
Arguments:
- block_input: bfloat16 [16384, 576], P(('rep', 'shard')), may hold values from -6 to 6
- w_query: bfloat16 [576, 576], P('shard'), may hold values from -0.25 to 0.25
- w_key: bfloat16 [576, 192], P('shard'), may hold values from -0.25 to 0.25
- w_value: bfloat16 [576, 192], P('shard'), may hold values from -0.25 to 0.25
- w_out: bfloat16 [576, 576], P('shard'), may hold values from -1 to 1
- w_gate: bfloat16 [576, 1536], P('shard'), may hold values from -0.25 to 0.25
- w_up: bfloat16 [576, 1536], P('shard'), may hold values from -0.25 to 0.25
- w_down: bfloat16 [1536, 576], P('shard'), may hold values from -0.15625 to 0.15625
- gain_attn: bfloat16 [576], P('shard'), may hold values from 0.5 to 1.5
- gain_ffn: bfloat16 [576], P('shard'), may hold values from 0.5 to 1.5
- cotangent: bfloat16 [16384, 576], P(('rep', 'shard')), may hold values from -12 to 12
Outputs:
- output: bfloat16 [16384, 576], P(('rep', 'shard'))
- grad_input: bfloat16 [16384, 576], P(('rep', 'shard'))
- grad_w_query: float32 [576, 576], P('shard')
- grad_w_key: float32 [576, 192], P('shard')
- grad_w_value: float32 [576, 192], P('shard')
- grad_w_out: float32 [576, 576], P('shard')
- grad_w_gate: float32 [576, 1536], P('shard')
- grad_w_up: float32 [576, 1536], P('shard')
- grad_w_down: float32 [1536, 576], P('shard')
- grad_gain_attn: float32 [576], P('shard')
- grad_gain_ffn: float32 [576], P('shard')
The draws below stay inside these ranges and needn't reach their ends.
All inputs are finite; a program needn't handle non-finite values.
Results may differ from the reference program's by a relative error of at most 0.017.
Values may be sent and summed in bfloat16 or wider, within the bound.
A program may use at most 128 MiB of HBM per device.

```python
import math
import jax
import jax.numpy as jnp
from jax import lax

D = 576
FF = 1536
HEADS = 9
KV_HEADS = 3
HEAD_DIM = 64
LEN = 512
KVD = 192
ROWS = 512
TOKENS = 16384
DEVICES = 32


def draw_cotangent(key, part):
    seq_count = TOKENS // LEN
    first, second = jax.random.split(jax.random.fold_in(key, 11), 2)
    scales = jnp.exp(jax.random.uniform(first, (seq_count, 1, 1), jnp.float32, math.log(0.3), math.log(3.0)))
    noise = jnp.clip(jax.random.normal(second, (seq_count, LEN, D), jnp.float32), -4.0, 4.0)
    return jnp.clip(noise * scales, -12.0, 12.0).reshape(TOKENS, D).astype(jnp.bfloat16)


def level_of(key, shape, cuts, low, high):
    level, own = 1.0, jax.random.fold_in(key, 6)
    for position, shards_of in cuts:
        heights = jnp.exp(jax.random.uniform(jax.random.fold_in(own, position), (shards_of,), jnp.float32, low / len(cuts), high / len(cuts)))
        level = level * jnp.repeat(heights, shape[position] // shards_of).reshape([-1 if axis == position else 1 for axis in range(len(shape))])
    return level


def gaussian(own_key, shape, scale, most, pieces=(), dtype=jnp.bfloat16):
    values = scale * jax.random.normal(own_key, shape, jnp.float32)
    if pieces:
        values = values * level_of(own_key, shape, pieces, -0.22, 0.18)
    return jnp.clip(values, -most, most).astype(dtype)


def setup_inputs(seed: int = 0) -> dict:
    key_of = jax.random.split(jax.random.key(seed), 12)
    return {
        "block_input": gaussian(key_of[0], (TOKENS, D), 1.0, 6.0, ((0, 32),)),
        "w_query": gaussian(key_of[1], (D, D), D ** -0.5, 0.25, ((0, 4),)),
        "w_key": gaussian(key_of[2], (D, KVD), D ** -0.5, 0.25, ((0, 4),)),
        "w_value": gaussian(key_of[3], (D, KVD), D ** -0.5, 0.25, ((0, 4),)),
        "w_out": gaussian(key_of[4], (D, D), (max(D // 16, 1)) ** -0.5, 1.0, ((0, 4),)),
        "w_gate": gaussian(key_of[5], (D, FF), D ** -0.5, 0.25, ((0, 4),)),
        "w_up": gaussian(key_of[6], (D, FF), D ** -0.5, 0.25, ((0, 4),)),
        "w_down": gaussian(key_of[7], (FF, D), FF ** -0.5, 0.15625, ((0, 4),)),
        "gain_attn": jnp.clip(1.0 + 0.1 * jax.random.normal(key_of[8], (D,), jnp.float32), 0.5, 1.5).astype(jnp.bfloat16),
        "gain_ffn": jnp.clip(1.0 + 0.1 * jax.random.normal(key_of[9], (D,), jnp.float32), 0.5, 1.5).astype(jnp.bfloat16),
        "cotangent": draw_cotangent(jax.random.fold_in(key_of[11], 71), 0),
    }


EPS = 1e-05
THETA = 100000.0

def product(left, right):
    return jnp.dot(left, right, preferred_element_type=jnp.float32)

def product_tn(left, right):
    return lax.dot_general(left, right, (((0,), (0,)), ((), ())), preferred_element_type=jnp.float32)

def product_nt(left, right):
    return lax.dot_general(left, right, (((1,), (1,)), ((), ())), preferred_element_type=jnp.float32)

def contract(form, left, right):
    return jnp.einsum(form, left.astype(jnp.float32), right.astype(jnp.float32))

def tables():
    half_dim = HEAD_DIM // 2
    ladder = jnp.arange(half_dim).astype(jnp.float32) * (2.0 / HEAD_DIM)
    freqs = jnp.power(THETA, -ladder)
    places = jnp.arange(LEN).astype(jnp.float32)
    angles = places[:, None] * freqs[None, :]
    angles = jnp.concatenate([angles, angles], axis=1)
    return (jnp.cos(angles), jnp.sin(angles))

def rotate(values, cosine, sine):
    half_dim = values.shape[-1] // 2
    turned = jnp.concatenate([-values[..., half_dim:], values[..., :half_dim]], axis=-1)
    return values * cosine[None, :, None, :] + turned * sine[None, :, None, :]

def unrotate(grads, cosine, sine):
    half_dim = grads.shape[-1] // 2
    scaled = grads * sine[None, :, None, :]
    turned = jnp.concatenate([scaled[..., half_dim:], -scaled[..., :half_dim]], axis=-1)
    return grads * cosine[None, :, None, :] + turned

def norm_forward(values, gain):
    scaling = lax.rsqrt(lax.optimization_barrier(jnp.mean(values * values, axis=-1, keepdims=True)) + EPS)
    unit_rows = values * scaling
    return (unit_rows, scaling, (unit_rows * gain[None, :]).astype(jnp.bfloat16))

def norm_backward(grads, unit_rows, scaling, gain):
    gain_grad = lax.optimization_barrier(jnp.sum(grads * unit_rows, axis=0))
    weighted = grads * gain[None, :]
    result = scaling * (weighted - unit_rows * lax.optimization_barrier(jnp.mean(weighted * unit_rows, axis=-1, keepdims=True)))
    return (result, gain_grad)

def masked_scores(query, keys):
    scores = contract('qkgd,skd->kgqs', query, keys) * (1.0 / math.sqrt(HEAD_DIM))
    row_ids = lax.broadcasted_iota(jnp.int32, (LEN, LEN), 0)
    col_ids = lax.broadcasted_iota(jnp.int32, (LEN, LEN), 1)
    return jnp.where((col_ids <= row_ids)[None, None], scores, -1e+30)

def attend_one(packed):
    query, keys, values = packed
    scores = masked_scores(query, keys)
    highest = lax.optimization_barrier(jnp.max(scores, axis=-1, keepdims=True))
    weights = jnp.exp(scores - highest)
    totals = lax.optimization_barrier(jnp.sum(weights, axis=-1, keepdims=True))
    log_sum = (highest + jnp.log(totals))[..., 0]
    probs = (weights / totals).astype(jnp.bfloat16)
    mixed = contract('kgqs,skd->qkgd', probs, values)
    return (mixed.astype(jnp.bfloat16), log_sum)

def attend_back(packed):
    query, keys, values, mixed, log_sum, grad_mixed = packed
    scores = masked_scores(query, keys)
    probs_full = jnp.exp(scores - log_sum[..., None])
    probs = probs_full.astype(jnp.bfloat16)
    grad_values = contract('kgqs,qkgd->skd', probs, grad_mixed)
    grad_probs = contract('qkgd,skd->kgqs', grad_mixed, values)
    delta = lax.optimization_barrier(jnp.sum(grad_mixed.astype(jnp.float32) * mixed.astype(jnp.float32), axis=-1))
    delta = jnp.transpose(delta, (1, 2, 0))
    grad_scores = (probs_full * (grad_probs - delta[..., None]) * (1.0 / math.sqrt(HEAD_DIM))).astype(jnp.bfloat16)
    grad_query = contract('kgqs,skd->qkgd', grad_scores, keys)
    grad_keys = contract('kgqs,qkgd->skd', grad_scores, query)
    return (grad_query, grad_keys, grad_values)

def forward(block_input, weights):
    w_query, w_key, w_value, w_out, w_gate, w_up, w_down, gain_attn, gain_ffn = weights
    rows = block_input.shape[0]
    seqs = rows // LEN
    group = HEADS // KV_HEADS
    cosine, sine = tables()
    residual = block_input.astype(jnp.float32)
    unit_one, scale_one, normed_one = norm_forward(residual, gain_attn.astype(jnp.float32))
    query = rotate(product(normed_one, w_query).reshape(seqs, LEN, HEADS, HEAD_DIM), cosine, sine)
    query = query.astype(jnp.bfloat16).reshape(seqs, LEN, KV_HEADS, group, HEAD_DIM)
    keys = rotate(product(normed_one, w_key).reshape(seqs, LEN, KV_HEADS, HEAD_DIM), cosine, sine).astype(jnp.bfloat16)
    values = product(normed_one, w_value).astype(jnp.bfloat16).reshape(seqs, LEN, KV_HEADS, HEAD_DIM)
    mixed, log_sum = lax.map(attend_one, (query, keys, values))
    attended = mixed.reshape(rows, D)
    middle = residual + product(attended, w_out)
    unit_two, scale_two, normed_two = norm_forward(middle, gain_ffn.astype(jnp.float32))
    gate_pre = product(normed_two, w_gate)
    up_pre = product(normed_two, w_up)
    hidden = (gate_pre * jax.nn.sigmoid(gate_pre) * up_pre).astype(jnp.bfloat16)
    output = (middle + product(hidden, w_down)).astype(jnp.bfloat16)
    state = (unit_one, scale_one, normed_one, query, keys, values, mixed, log_sum, attended, unit_two, scale_two, normed_two, gate_pre, up_pre, hidden)
    return (output, state)

def backward(state, cotangent, weights):
    w_query, w_key, w_value, w_out, w_gate, w_up, w_down, gain_attn, gain_ffn = weights
    unit_one, scale_one, normed_one, query, keys, values, mixed, log_sum, attended, unit_two, scale_two, normed_two, gate_pre, up_pre, hidden = state
    rows = cotangent.shape[0]
    seqs = rows // LEN
    group = HEADS // KV_HEADS
    cosine, sine = tables()
    grad_hidden = product_nt(cotangent, w_down)
    sigmoid = jax.nn.sigmoid(gate_pre)
    grad_gate = (grad_hidden * up_pre * sigmoid * (1.0 + gate_pre * (1.0 - sigmoid))).astype(jnp.bfloat16)
    grad_up = (grad_hidden * gate_pre * sigmoid).astype(jnp.bfloat16)
    grad_normed_two = product_nt(grad_gate, w_gate) + product_nt(grad_up, w_up)
    back_two, gain_two_grad = norm_backward(grad_normed_two, unit_two, scale_two, gain_ffn.astype(jnp.float32))
    grad_middle = cotangent.astype(jnp.float32) + back_two
    grad_middle_low = grad_middle.astype(jnp.bfloat16)
    grad_attended = product_nt(grad_middle_low, w_out).astype(jnp.bfloat16)
    grad_attended = grad_attended.reshape(seqs, LEN, KV_HEADS, group, HEAD_DIM)
    grad_query, grad_keys, grad_values = lax.map(attend_back, (query, keys, values, mixed, log_sum, grad_attended))
    grad_query = unrotate(grad_query.reshape(seqs, LEN, HEADS, HEAD_DIM), cosine, sine)
    grad_query = grad_query.astype(jnp.bfloat16).reshape(rows, D)
    grad_keys = unrotate(grad_keys, cosine, sine).astype(jnp.bfloat16).reshape(rows, KVD)
    grad_values = grad_values.astype(jnp.bfloat16).reshape(rows, KVD)
    grad_normed_one = product_nt(grad_query, w_query) + product_nt(grad_keys, w_key) + product_nt(grad_values, w_value)
    back_one, gain_one_grad = norm_backward(grad_normed_one, unit_one, scale_one, gain_attn.astype(jnp.float32))
    grad_input = (grad_middle + back_one).astype(jnp.bfloat16)
    partials = (product_tn(normed_one, grad_query), product_tn(normed_one, grad_keys), product_tn(normed_one, grad_values), product_tn(attended, grad_middle_low), product_tn(normed_two, grad_gate), product_tn(normed_two, grad_up), product_tn(hidden, cotangent), gain_one_grad, gain_two_grad)
    return (grad_input, partials)

def reference(block_input, w_query, w_key, w_value, w_out, w_gate, w_up, w_down, gain_attn, gain_ffn, cotangent):
    weights = (w_query, w_key, w_value, w_out, w_gate, w_up, w_down, gain_attn, gain_ffn)
    inputs = block_input.reshape(DEVICES, ROWS, D)
    cotangents = cotangent.reshape(DEVICES, ROWS, D)

    def visit(running, pair):
        output, state = forward(pair[0], weights)
        grad_input, partials = backward(state, pair[1], weights)
        running = tuple((accum + lax.optimization_barrier(piece_grad.astype(jnp.bfloat16)).astype(jnp.float32) for accum, piece_grad in zip(running, partials)))
        return (running, (output, grad_input))
    start = tuple((jnp.zeros(weight.shape, jnp.float32) for weight in weights))
    sums, (outputs, grads) = lax.scan(visit, start, (inputs, cotangents))
    return (outputs.reshape(TOKENS, D), grads.reshape(TOKENS, D), sums[0], sums[1], sums[2], sums[3], sums[4], sums[5], sums[6], sums[7], sums[8])
```

```python
import math

import jax
import jax.numpy as jnp
from jax import lax
from jax.experimental import pallas as pl
from jax.experimental.pallas import tpu as pltpu
from jax.sharding import PartitionSpec as P

D = 576
HEADS = 9
KV_HEADS = 3
HEAD_DIM = 64
LEN = 512
KVD = 192


EPS = 1e-05
THETA = 100000.0


def product(left, right):
    return jnp.dot(left, right, preferred_element_type=jnp.float32)


def product_tn(left, right):
    return lax.dot_general(
        left, right, (((0,), (0,)), ((), ())), preferred_element_type=jnp.float32
    )


def product_nt(left, right):
    return lax.dot_general(
        left, right, (((1,), (1,)), ((), ())), preferred_element_type=jnp.float32
    )


def contract(form, left, right):
    return jnp.einsum(form, left, right, preferred_element_type=jnp.float32)


def tables():
    half_dim = HEAD_DIM // 2
    ladder = jnp.arange(half_dim).astype(jnp.float32) * (2.0 / HEAD_DIM)
    freqs = jnp.power(THETA, -ladder)
    places = jnp.arange(LEN).astype(jnp.float32)
    angles = places[:, None] * freqs[None, :]
    angles = jnp.concatenate([angles, angles], axis=1)
    return (jnp.cos(angles), jnp.sin(angles))


def rotate(values, cosine, sine):
    half_dim = values.shape[-1] // 2
    turned = jnp.concatenate([-values[..., half_dim:], values[..., :half_dim]], axis=-1)
    return values * cosine[None, :, None, :] + turned * sine[None, :, None, :]


def unrotate(grads, cosine, sine):
    half_dim = grads.shape[-1] // 2
    scaled = grads * sine[None, :, None, :]
    turned = jnp.concatenate([scaled[..., half_dim:], -scaled[..., :half_dim]], axis=-1)
    return grads * cosine[None, :, None, :] + turned


def norm_forward(values, gain):
    scaling = lax.rsqrt(jnp.mean(values * values, axis=-1, keepdims=True) + EPS)
    unit_rows = values * scaling
    return (unit_rows, scaling, (unit_rows * gain[None, :]).astype(jnp.bfloat16))


def norm_backward(grads, unit_rows, scaling, gain):
    gain_grad = jnp.sum(grads * unit_rows, axis=0)
    weighted = grads * gain[None, :]
    result = scaling * (
        weighted - unit_rows * jnp.mean(weighted * unit_rows, axis=-1, keepdims=True)
    )
    return (result, gain_grad)


def masked_scores(query, keys):
    scores = contract("qkgd,skd->kgqs", query, keys) * (1.0 / math.sqrt(HEAD_DIM))
    row_ids = lax.broadcasted_iota(jnp.int32, (LEN, LEN), 0)
    col_ids = lax.broadcasted_iota(jnp.int32, (LEN, LEN), 1)
    return jnp.where((col_ids <= row_ids)[None, None], scores, -1e30)


def attend_one(packed):
    query, keys, values = packed
    scores = masked_scores(query, keys)
    highest = jnp.max(scores, axis=-1, keepdims=True)
    weights = jnp.exp(scores - highest)
    totals = jnp.sum(weights, axis=-1, keepdims=True)
    log_sum = (highest + jnp.log(totals))[..., 0]
    probs = (weights / totals).astype(jnp.bfloat16)
    mixed = contract("kgqs,skd->qkgd", probs, values)
    return (mixed.astype(jnp.bfloat16), log_sum)


def attend_back(packed):
    query, keys, values, mixed, log_sum, grad_mixed = packed
    scores = masked_scores(query, keys)
    probs_full = jnp.exp(scores - log_sum[..., None])
    probs = probs_full.astype(jnp.bfloat16)
    grad_values = contract("kgqs,qkgd->skd", probs, grad_mixed)
    grad_probs = contract("qkgd,skd->kgqs", grad_mixed, values)
    delta = jnp.sum(grad_mixed.astype(jnp.float32) * mixed.astype(jnp.float32), axis=-1)
    delta = jnp.transpose(delta, (1, 2, 0))
    grad_scores = (
        probs_full * (grad_probs - delta[..., None]) * (1.0 / math.sqrt(HEAD_DIM))
    ).astype(jnp.bfloat16)
    grad_query = contract("kgqs,skd->qkgd", grad_scores, keys)
    grad_keys = contract("kgqs,qkgd->skd", grad_scores, query)
    return (grad_query, grad_keys, grad_values)


def forward(block_input, weights):
    w_qkv, w_out, w_gate, w_up, w_down_t, gain_attn, gain_ffn = weights
    rows = block_input.shape[0]
    seqs = rows // LEN
    group = HEADS // KV_HEADS
    cosine, sine = tables()
    residual = block_input.astype(jnp.float32)
    unit_one, scale_one, normed_one = norm_forward(residual, gain_attn.astype(jnp.float32))
    projected = product(normed_one, w_qkv)
    query = rotate(projected[:, :D].reshape(seqs, LEN, HEADS, HEAD_DIM), cosine, sine)
    query = query.astype(jnp.bfloat16).reshape(seqs, LEN, KV_HEADS, group, HEAD_DIM)
    keys = rotate(
        projected[:, D : D + KVD].reshape(seqs, LEN, KV_HEADS, HEAD_DIM), cosine, sine
    ).astype(jnp.bfloat16)
    values = (
        projected[:, D + KVD :].astype(jnp.bfloat16).reshape(seqs, LEN, KV_HEADS, HEAD_DIM)
    )
    mixed, log_sum = lax.map(attend_one, (query, keys, values))
    attended = mixed.reshape(rows, D)
    middle = residual + product(attended, w_out)
    unit_two, scale_two, normed_two = norm_forward(middle, gain_ffn.astype(jnp.float32))
    gate_pre = product(normed_two, w_gate)
    up_pre = product(normed_two, w_up)
    hidden = (gate_pre * jax.nn.sigmoid(gate_pre) * up_pre).astype(jnp.bfloat16)
    output = (middle + product_nt(hidden, w_down_t)).astype(jnp.bfloat16)
    state = (
        unit_one,
        scale_one,
        normed_one,
        query,
        keys,
        values,
        mixed,
        log_sum,
        attended,
        unit_two,
        scale_two,
        normed_two,
        gate_pre,
        up_pre,
        hidden,
    )
    return (output, state)


def backward(state, cotangent, weights):
    w_qkv, w_out, w_gate, w_up, w_down_t, gain_attn, gain_ffn = weights
    (
        unit_one,
        scale_one,
        normed_one,
        query,
        keys,
        values,
        mixed,
        log_sum,
        attended,
        unit_two,
        scale_two,
        normed_two,
        gate_pre,
        up_pre,
        hidden,
    ) = state
    rows = cotangent.shape[0]
    seqs = rows // LEN
    group = HEADS // KV_HEADS
    cosine, sine = tables()
    grad_hidden = product(cotangent, w_down_t)
    sigmoid = jax.nn.sigmoid(gate_pre)
    grad_gate = (grad_hidden * up_pre * sigmoid * (1.0 + gate_pre * (1.0 - sigmoid))).astype(
        jnp.bfloat16
    )
    grad_up = (grad_hidden * gate_pre * sigmoid).astype(jnp.bfloat16)
    grad_normed_two = product_nt(grad_gate, w_gate) + product_nt(grad_up, w_up)
    back_two, gain_two_grad = norm_backward(
        grad_normed_two, unit_two, scale_two, gain_ffn.astype(jnp.float32)
    )
    grad_middle = cotangent.astype(jnp.float32) + back_two
    grad_middle_low = grad_middle.astype(jnp.bfloat16)
    grad_attended = product_nt(grad_middle_low, w_out).astype(jnp.bfloat16)
    grad_attended = grad_attended.reshape(seqs, LEN, KV_HEADS, group, HEAD_DIM)
    grad_query, grad_keys, grad_values = lax.map(
        attend_back, (query, keys, values, mixed, log_sum, grad_attended)
    )
    grad_query = unrotate(grad_query.reshape(seqs, LEN, HEADS, HEAD_DIM), cosine, sine)
    grad_query = grad_query.astype(jnp.bfloat16).reshape(rows, D)
    grad_keys = unrotate(grad_keys, cosine, sine).astype(jnp.bfloat16).reshape(rows, KVD)
    grad_values = grad_values.astype(jnp.bfloat16).reshape(rows, KVD)
    grad_normed_one = product_nt(
        jnp.concatenate([grad_query, grad_keys, grad_values], axis=1), w_qkv
    )
    back_one, gain_one_grad = norm_backward(
        grad_normed_one, unit_one, scale_one, gain_attn.astype(jnp.float32)
    )
    grad_input = (grad_middle + back_one).astype(jnp.bfloat16)
    operands = (
        cotangent,
        hidden,
        normed_two,
        grad_gate,
        grad_up,
        normed_one,
        attended,
        jnp.concatenate([grad_query, grad_keys, grad_values], axis=1),
        grad_middle_low,
        gain_one_grad,
        gain_two_grad,
    )
    return (grad_input, operands)


MESH = pl.DeviceIdType.MESH
LOW = 8


def place(shard_count):
    rep = lax.axis_index("rep")
    shard = lax.axis_index("shard")
    low = rep % LOW
    return rep, shard, low


def flipped(index, step):
    bit = (index // step) % 2
    return index + step - 2 * step * bit


def greet(rep, shard, reps, shard_count):
    barrier = pltpu.get_barrier_semaphore()
    met = 0
    step = 1
    while step < reps:
        pl.semaphore_signal(
            barrier, inc=1, device_id=(flipped(rep, step), shard), device_id_type=MESH
        )
        met += 1
        step *= 2
    for ahead in range(1, shard_count):
        pl.semaphore_signal(
            barrier, inc=1, device_id=(rep, (shard + ahead) % shard_count), device_id_type=MESH
        )
        met += 1
    pl.semaphore_wait(barrier, met)


def remote(source, target, sems, index, device):
    return pltpu.make_async_remote_copy(
        src_ref=source,
        dst_ref=target,
        send_sem=sems[0].at[index],
        recv_sem=sems[1].at[index],
        device_id=device,
        device_id_type=MESH,
    )


def steps_of(half):
    return (4, 2) if half == 0 else (2, 4)


def gather_kernel(
    shard_count, own, gains, down, gate, up, rest, all_gains, buf, zs, zr, ps, pr, gs, gr, outs
):
    rep, shard, low = place(shard_count)
    greet(rep, shard, LOW, shard_count)
    finals = (down, gate, up, rest)
    rows, cols = own.shape[2:]

    def put(source, owner, chunk, half, index):
        final = finals[chunk // 2]
        lane = 2 * (chunk % 2) + half
        if chunk // 2 == 0:
            where = final.at[
                pl.ds(lane * rows, rows), pl.ds(pl.multiple_of(owner * cols, 128), cols)
            ]
        else:
            where = final.at[
                pl.ds(pl.multiple_of(owner * rows, 16), rows), pl.ds(lane * cols, cols)
            ]
        copy = pltpu.make_async_copy(source, where, outs.at[index])
        copy.start()
        return copy

    sent = []
    landed = {}
    copies = []
    for ahead in range(1, shard_count):
        device = (rep, (shard + ahead) % shard_count)
        for half in range(2):
            copy = remote(
                own.at[low, half],
                buf.at[shard, low, half],
                (zs, zr),
                2 * ahead + half,
                device,
            )
            copy.start()
            landed[ahead, half] = copy
    gain_copies = []
    for ahead in range(1, shard_count):
        device = (rep, (shard + ahead) % shard_count)
        copy = remote(gains, all_gains.at[shard], (gs, gr), ahead, device)
        copy.start()
        gain_copies.append(copy)
    all_gains[shard] = gains[...]
    for chunk in range(LOW):
        for half in range(2):
            copies.append(put(own.at[chunk, half], shard, chunk, half, 2 * chunk + half))

    pieces = [(ahead, half) for ahead in range(1, shard_count) for half in range(2)]
    base = {piece: 7 * number for number, piece in enumerate(pieces)}
    core = flipped(rep, 1)
    jobs = {}

    def pass_on(piece, slot, chunk, partner):
        ahead, half = piece
        owner = (shard + shard_count - ahead) % shard_count
        copy = remote(
            buf.at[owner, chunk, half],
            buf.at[owner, chunk, half],
            (ps, pr),
            base[piece] + slot,
            (partner, shard),
        )
        copy.start()
        jobs[piece, slot] = copy

    for piece in pieces:
        first, second = steps_of(piece[1])
        landed[piece].wait_recv()
        pass_on(piece, 0, low, flipped(rep, first))
        pass_on(piece, 1, low, flipped(rep, second))
        pass_on(piece, 3, low, core)
    for piece in pieces:
        first, second = steps_of(piece[1])
        jobs[piece, 0].wait_recv()
        pass_on(piece, 2, flipped(low, first), flipped(rep, second))
        pass_on(piece, 4, flipped(low, first), core)
    for piece in pieces:
        first, second = steps_of(piece[1])
        jobs[piece, 1].wait_recv()
        pass_on(piece, 5, flipped(low, second), core)
        jobs[piece, 2].wait_recv()
        pass_on(piece, 6, flipped(flipped(low, first), second), core)
    for number, piece in enumerate(pieces):
        ahead, half = piece
        owner = (shard + shard_count - ahead) % shard_count
        for slot in range(3, 7):
            jobs[piece, slot].wait_recv()
        for chunk in range(LOW):
            index = 2 * LOW + LOW * number + chunk
            copies.append(put(buf.at[owner, chunk, half], owner, chunk, half, index))
    for copy in landed.values():
        copy.wait_send()
    for copy in jobs.values():
        copy.wait_send()
    for copy in gain_copies:
        copy.wait()
    for copy in copies:
        copy.wait()


def pack(mats):
    down_t = mats[0]
    rows, cols = down_t.shape[0] // 4, down_t.shape[1]
    parts = [down_t.reshape(4, rows, cols)]
    for mat in mats[1:]:
        parts.append(jnp.stack([mat[:, i * cols : (i + 1) * cols] for i in range(4)]))
    return jnp.stack(parts).reshape(LOW, 2, rows, cols)


def gain_tile(first, second):
    flat = jnp.concatenate([first, second], axis=-1).astype(jnp.float32)
    pad = [(0, 0)] * (flat.ndim - 1) + [(0, 8 * 128 - flat.shape[-1])]
    return jnp.pad(flat, pad).reshape(flat.shape[:-1] + (8, 128))


def gather(own, gains, shard_count):
    rows, cols = own.shape[2:]
    full = jax.ShapeDtypeStruct((shard_count * rows, 4 * cols), jnp.bfloat16)
    full_down = jax.ShapeDtypeStruct((4 * rows, shard_count * cols), jnp.bfloat16)
    moves = 2 * shard_count
    hops = 14 * (shard_count - 1)
    dma = pltpu.SemaphoreType.DMA
    return pl.pallas_call(
        lambda *refs: gather_kernel(shard_count, *refs),
        name="gather_weights",
        out_shape=(
            full_down,
            full,
            full,
            full,
            jax.ShapeDtypeStruct((shard_count, 8, 128), jnp.float32),
        ),
        in_specs=[pl.BlockSpec(memory_space=pltpu.VMEM)] * 2,
        out_specs=tuple(
            [pl.BlockSpec(memory_space=pl.ANY)] * 4 + [pl.BlockSpec(memory_space=pltpu.VMEM)]
        ),
        scratch_shapes=[
            pltpu.VMEM((shard_count, LOW, 2, rows, cols), jnp.bfloat16),
            dma((moves,)),
            dma((moves,)),
            dma((hops,)),
            dma((hops,)),
            dma((shard_count,)),
            dma((shard_count,)),
            dma((2 * LOW * shard_count,)),
        ],
        compiler_params=pltpu.CompilerParams(collective_id=0, has_side_effects=True),
    )(own, gains)


def add_low(left, right):
    return (left.astype(jnp.float32) + right.astype(jnp.float32)).astype(jnp.bfloat16)


def reduce_kernel(
    reps,
    shard_count,
    cot,
    hidden,
    normed,
    grad_gate,
    grad_up,
    left,
    right,
    gains,
    total,
    gain_total,
    grads,
    core_in,
    one_in,
    two_in,
    shard_in,
    late_out,
    late_in,
    gain_work,
    gain_in,
    gain_shard_in,
    cs,
    cr,
    os,
    orr,
    ts,
    tr,
    zs,
    zr,
    ls,
    lr,
    ps,
    pr,
    gs,
    gr,
):
    rep, shard, low = place(shard_count)
    greet(rep, shard, reps, shard_count)
    rows, cols = total.shape[2:]
    core = flipped(rep, 1)
    mine = low % 2
    order = list(range(1, shard_count)) + [0]
    copies = []

    def owner_of(ahead):
        return (shard + ahead) % shard_count

    gain_steps = []
    step = 1
    while step < reps:
        gain_steps.append(step)
        step *= 2

    def gain_send(number):
        copy = remote(
            gain_work.at[number],
            gain_in.at[number],
            (gs, gr),
            number,
            (flipped(rep, gain_steps[number]), shard),
        )
        copy.start()
        return copy

    def gain_take(number, copy):
        copy.wait_recv()
        gain_work[number + 1] = gain_work[number] + gain_in[number]
        copies.append(copy)

    gain_work[0] = gains[...]
    gain_copy = gain_send(0)

    swaps = {}
    for matrix in range(4):
        if matrix == 0:
            turned = cot[...].T
            for owner in range(shard_count):
                product_here = jnp.dot(
                    turned,
                    hidden[:, owner * cols : (owner + 1) * cols],
                    preferred_element_type=jnp.float32,
                )
                for lane in range(4):
                    grads[owner, lane // 2, lane % 2] = product_here[
                        lane * rows : (lane + 1) * rows
                    ].astype(jnp.bfloat16)
        else:
            lhs, rhs = ((normed, grad_gate), (normed, grad_up), (left, right))[matrix - 1]
            turned = lhs[...].T
            for lane in range(4):
                product_here = jnp.dot(
                    turned,
                    rhs[:, lane * cols : (lane + 1) * cols],
                    preferred_element_type=jnp.float32,
                )
                for owner in range(shard_count):
                    grads[owner, 2 * matrix + lane // 2, lane % 2] = product_here[
                        owner * rows : (owner + 1) * rows
                    ].astype(jnp.bfloat16)
        for ahead in order:
            copy = remote(
                grads.at[owner_of(ahead), 2 * matrix + 1 - mine],
                core_in.at[matrix, ahead],
                (cs, cr),
                matrix * shard_count + ahead,
                (core, shard),
            )
            copy.start()
            swaps[matrix, ahead] = copy
            copies.append(copy)
        if matrix + 1 < len(gain_steps):
            gain_take(matrix, gain_copy)
            gain_copy = gain_send(matrix + 1)

    for number in range(min(4, len(gain_steps) - 1), len(gain_steps)):
        gain_take(number, gain_copy)
        if number + 1 < len(gain_steps):
            gain_copy = gain_send(number + 1)
    tail = len(gain_steps)
    gain_shards = {}
    for ahead in range(1, shard_count):
        copy = remote(
            gain_work.at[tail, owner_of(ahead)],
            gain_shard_in.at[ahead],
            (gs, gr),
            tail + ahead,
            (rep, owner_of(ahead)),
        )
        copy.start()
        gain_shards[ahead] = copy
        copies.append(copy)

    high, mid = low // 4, (low // 2) % 2
    ones = {}
    for ahead in order:
        owner = owner_of(ahead)
        for matrix in range(4):
            swaps[matrix, ahead].wait_recv()
            for half in range(2):
                grads[owner, 2 * matrix + mine, half] = add_low(
                    grads[owner, 2 * matrix + mine, half], core_in[matrix, ahead, half]
                )
        for half in range(2):
            for other in range(2):
                if half == 0:
                    matrix = 2 * (1 - high) + other
                else:
                    matrix = 2 * other + 1 - mid
                copy = remote(
                    grads.at[owner, 2 * matrix + mine, half],
                    one_in.at[ahead, half, other],
                    (os, orr),
                    4 * ahead + 2 * half + other,
                    (flipped(rep, steps_of(half)[0]), shard),
                )
                copy.start()
                ones[ahead, half, other] = copy
                copies.append(copy)
    twos = {}
    for ahead in order:
        owner = owner_of(ahead)
        for half in range(2):
            for other in range(2):
                ones[ahead, half, other].wait_recv()
                matrix = 2 * high + other if half == 0 else 2 * other + mid
                grads[owner, 2 * matrix + mine, half] = add_low(
                    grads[owner, 2 * matrix + mine, half], one_in[ahead, half, other]
                )
            matrix = 2 * high + 1 - mid if half == 0 else 2 * (1 - high) + mid
            copy = remote(
                grads.at[owner, 2 * matrix + mine, half],
                two_in.at[ahead, half],
                (ts, tr),
                2 * ahead + half,
                (flipped(rep, steps_of(half)[1]), shard),
            )
            copy.start()
            twos[ahead, half] = copy
            copies.append(copy)
    lands = {}
    for ahead in order:
        owner = owner_of(ahead)
        for half in range(2):
            twos[ahead, half].wait_recv()
            grads[owner, low, half] = add_low(grads[owner, low, half], two_in[ahead, half])
            if ahead:
                copy = remote(
                    grads.at[owner, low, half],
                    shard_in.at[ahead, half],
                    (zs, zr),
                    2 * ahead + half,
                    (rep, owner),
                )
                copy.start()
                lands[ahead, half] = copy
                copies.append(copy)

    jobs = {}

    def pass_on(half, slot, chunk, partner):
        copy = remote(
            total.at[chunk, half],
            total.at[chunk, half],
            (ps, pr),
            7 * half + slot,
            (partner, shard),
        )
        copy.start()
        jobs[half, slot] = copy
        copies.append(copy)

    for half in range(2):
        first, second = steps_of(half)
        running = grads[shard, low, half].astype(jnp.float32)
        for ahead in range(1, shard_count):
            lands[ahead, half].wait_recv()
            running = running + shard_in[ahead, half].astype(jnp.float32)
        step, number = LOW, 0
        while step < reps:
            late_out[number, half] = running.astype(jnp.bfloat16)
            copy = remote(
                late_out.at[number, half],
                late_in.at[number, half],
                (ls, lr),
                2 * number + half,
                (flipped(rep, step), shard),
            )
            copy.start()
            copy.wait_recv()
            copies.append(copy)
            running = late_out[number, half].astype(jnp.float32) + late_in[
                number, half
            ].astype(jnp.float32)
            step, number = 2 * step, number + 1
        total[low, half] = running.astype(jnp.bfloat16)
        pass_on(half, 0, low, flipped(rep, first))
        pass_on(half, 1, low, flipped(rep, second))
        pass_on(half, 3, low, core)
    running = gain_work[tail, shard]
    for ahead in range(1, shard_count):
        gain_shards[ahead].wait_recv()
        running = running + gain_shard_in[ahead]
    gain_total[...] = running
    for half in range(2):
        first, second = steps_of(half)
        jobs[half, 0].wait_recv()
        pass_on(half, 2, flipped(low, first), flipped(rep, second))
        pass_on(half, 4, flipped(low, first), core)
    for half in range(2):
        first, second = steps_of(half)
        jobs[half, 1].wait_recv()
        pass_on(half, 5, flipped(low, second), core)
        jobs[half, 2].wait_recv()
        pass_on(half, 6, flipped(flipped(low, first), second), core)
    for half in range(2):
        for slot in range(3, 7):
            jobs[half, slot].wait_recv()
    for copy in copies:
        copy.wait_send()


def reduce_all(operands, reps, shard_count):
    cot, hidden, normed, grad_gate, grad_up, left, right, gains = operands
    rows, cols = D // 4, hidden.shape[1] // 4
    dma = pltpu.SemaphoreType.DMA
    low = jnp.bfloat16
    bits = reps.bit_length() - 1
    late = max(bits - 3, 1)
    sems = []
    for count in (
        4 * shard_count,
        4 * shard_count,
        2 * shard_count,
        2 * shard_count,
        2 * late,
        14,
        bits + shard_count,
    ):
        sems += [dma((count,)), dma((count,))]
    return pl.pallas_call(
        lambda *refs: reduce_kernel(reps, shard_count, *refs),
        name="reduce_grads",
        out_shape=(
            jax.ShapeDtypeStruct((LOW, 2, rows, cols), low),
            jax.ShapeDtypeStruct((8, 128), jnp.float32),
        ),
        in_specs=[pl.BlockSpec(memory_space=pltpu.VMEM)] * 8,
        out_specs=tuple([pl.BlockSpec(memory_space=pltpu.VMEM)] * 2),
        scratch_shapes=[
            pltpu.VMEM((shard_count, LOW, 2, rows, cols), low),
            pltpu.VMEM((4, shard_count, 2, rows, cols), low),
            pltpu.VMEM((shard_count, 2, 2, rows, cols), low),
            pltpu.VMEM((shard_count, 2, rows, cols), low),
            pltpu.VMEM((shard_count, 2, rows, cols), low),
            pltpu.VMEM((late, 2, rows, cols), low),
            pltpu.VMEM((late, 2, rows, cols), low),
            pltpu.VMEM((bits + 1, shard_count, 8, 128), jnp.float32),
            pltpu.VMEM((bits, shard_count, 8, 128), jnp.float32),
            pltpu.VMEM((shard_count, 8, 128), jnp.float32),
        ]
        + sems,
        compiler_params=pltpu.CompilerParams(
            collective_id=1, has_side_effects=True, vmem_limit_bytes=60000 * 1024
        ),
    )(cot, hidden, normed, grad_gate, grad_up, left, right, gains)


def shards(
    reps,
    shard_count,
    block_input,
    w_query,
    w_key,
    w_value,
    w_out,
    w_gate,
    w_up,
    w_down,
    gain_attn,
    gain_ffn,
    cotangent,
):
    rest = jnp.concatenate([w_query, w_key, w_value, w_out], axis=1)
    own = pack((w_down.T, w_gate, w_up, rest))
    full_down_t, full_gate, full_up, full_rest, tiles = gather(
        own, gain_tile(gain_attn, gain_ffn), shard_count
    )
    each = D // shard_count
    flat = tiles.reshape(shard_count, -1)
    full_gain_attn = flat[:, :each].reshape(-1)
    full_gain_ffn = flat[:, each : 2 * each].reshape(-1)
    width = D + 2 * KVD
    weights = (
        full_rest[:, :width],
        full_rest[:, width:],
        full_gate,
        full_up,
        full_down_t,
        full_gain_attn,
        full_gain_ffn,
    )
    output, state = forward(block_input, weights)
    grad_input, operands = backward(state, cotangent, weights)
    (
        cot,
        hidden,
        normed_two,
        grad_gate,
        grad_up,
        normed_one,
        attended,
        grad_qkv,
        grad_middle_low,
        gain_one_grad,
        gain_two_grad,
    ) = operands
    left = jnp.concatenate([normed_one, attended], axis=0)
    right = jnp.concatenate(
        [
            jnp.pad(grad_qkv, ((0, 0), (0, D))),
            jnp.pad(grad_middle_low, ((0, 0), (width, 0))),
        ],
        axis=0,
    )
    gains = gain_tile(
        gain_one_grad.reshape(shard_count, each), gain_two_grad.reshape(shard_count, each)
    )
    total, gain_total = reduce_all(
        (cot, hidden, normed_two, grad_gate, grad_up, left, right, gains), reps, shard_count
    )
    rows, cols = total.shape[2:]
    blocks = total.astype(jnp.float32).reshape(4, 4, rows, cols)

    def wide(matrix):
        return jnp.concatenate([blocks[matrix, lane] for lane in range(4)], axis=1)

    grad_rest = wide(3)
    sums = gain_total.reshape(-1)
    return (
        output,
        grad_input,
        grad_rest[:, :D],
        grad_rest[:, D : D + KVD],
        grad_rest[:, D + KVD : width],
        grad_rest[:, width:],
        wide(1),
        wide(2),
        blocks[0].reshape(4 * rows, cols).T,
        sums[:each],
        sums[each : 2 * each],
    )


def solution(mesh):
    placed = (
        P(("rep", "shard"), None),
        P("shard", None),
        P("shard", None),
        P("shard", None),
        P("shard", None),
        P("shard", None),
        P("shard", None),
        P("shard", None),
        P("shard"),
        P("shard"),
        P(("rep", "shard"), None),
    )
    return jax.shard_map(
        lambda *args: shards(mesh.shape["rep"], mesh.shape["shard"], *args),
        mesh=mesh,
        in_specs=placed,
        out_specs=(
            P(("rep", "shard"), None),
            P(("rep", "shard"), None),
            P("shard", None),
            P("shard", None),
            P("shard", None),
            P("shard", None),
            P("shard", None),
            P("shard", None),
            P("shard", None),
            P("shard"),
            P("shard"),
        ),
        check_vma=False,
    )
```

```python
import math

import jax
import jax.numpy as jnp
from jax import lax
from jax.experimental import pallas as pl
from jax.experimental.pallas import tpu as pltpu
from jax.sharding import PartitionSpec as P

D = 576
HEADS = 9
KV_HEADS = 3
HEAD_DIM = 64
LEN = 512
KVD = 192


EPS = 1e-05
THETA = 100000.0


def product(left, right):
    return jnp.dot(left, right, preferred_element_type=jnp.float32)


def product_tn(left, right):
    return lax.dot_general(
        left, right, (((0,), (0,)), ((), ())), preferred_element_type=jnp.float32
    )


def product_nt(left, right):
    return lax.dot_general(
        left, right, (((1,), (1,)), ((), ())), preferred_element_type=jnp.float32
    )


def contract(form, left, right):
    return jnp.einsum(form, left, right, preferred_element_type=jnp.float32)


def tables():
    half_dim = HEAD_DIM // 2
    ladder = jnp.arange(half_dim).astype(jnp.float32) * (2.0 / HEAD_DIM)
    freqs = jnp.power(THETA, -ladder)
    places = jnp.arange(LEN).astype(jnp.float32)
    angles = places[:, None] * freqs[None, :]
    angles = jnp.concatenate([angles, angles], axis=1)
    return (jnp.cos(angles), jnp.sin(angles))


def rotate(values, cosine, sine):
    half_dim = values.shape[-1] // 2
    turned = jnp.concatenate([-values[..., half_dim:], values[..., :half_dim]], axis=-1)
    return values * cosine[None, :, None, :] + turned * sine[None, :, None, :]


def norm_forward(values, gain):
    scaling = lax.rsqrt(jnp.mean(values * values, axis=-1, keepdims=True) + EPS)
    unit_rows = values * scaling
    return (unit_rows, scaling, (unit_rows * gain[None, :]).astype(jnp.bfloat16))


def norm_backward(grads, unit_rows, scaling, gain):
    gain_grad = jnp.sum(grads * unit_rows, axis=0)
    weighted = grads * gain[None, :]
    result = scaling * (
        weighted - unit_rows * jnp.mean(weighted * unit_rows, axis=-1, keepdims=True)
    )
    return (result, gain_grad)


def masked_scores(query, keys):
    scores = contract("qkgd,skd->kgqs", query, keys) * (1.0 / math.sqrt(HEAD_DIM))
    row_ids = lax.broadcasted_iota(jnp.int32, (LEN, LEN), 0)
    col_ids = lax.broadcasted_iota(jnp.int32, (LEN, LEN), 1)
    return jnp.where((col_ids <= row_ids)[None, None], scores, -1e30)


def attend_one(packed):
    query, keys, values = packed
    scores = masked_scores(query, keys)
    highest = jnp.max(scores, axis=-1, keepdims=True)
    weights = jnp.exp(scores - highest)
    totals = jnp.sum(weights, axis=-1, keepdims=True)
    log_sum = (highest + jnp.log(totals))[..., 0]
    probs = (weights / totals).astype(jnp.bfloat16)
    mixed = contract("kgqs,skd->qkgd", probs, values)
    return (mixed.astype(jnp.bfloat16), log_sum)


def forward(block_input, weights):
    w_qkv, w_out, w_gate, w_up, w_down_t, gain_attn, gain_ffn = weights
    rows = block_input.shape[0]
    seqs = rows // LEN
    group = HEADS // KV_HEADS
    cosine, sine = tables()
    residual = block_input.astype(jnp.float32)
    unit_one, scale_one, normed_one = norm_forward(residual, gain_attn.astype(jnp.float32))
    projected = product(normed_one, w_qkv)
    query = rotate(projected[:, :D].reshape(seqs, LEN, HEADS, HEAD_DIM), cosine, sine)
    query = query.astype(jnp.bfloat16).reshape(seqs, LEN, KV_HEADS, group, HEAD_DIM)
    keys = rotate(
        projected[:, D : D + KVD].reshape(seqs, LEN, KV_HEADS, HEAD_DIM), cosine, sine
    ).astype(jnp.bfloat16)
    values = (
        projected[:, D + KVD :].astype(jnp.bfloat16).reshape(seqs, LEN, KV_HEADS, HEAD_DIM)
    )
    mixed, log_sum = lax.map(attend_one, (query, keys, values))
    attended = mixed.reshape(rows, D)
    middle = residual + product(attended, w_out)
    unit_two, scale_two, normed_two = norm_forward(middle, gain_ffn.astype(jnp.float32))
    gate_pre = product(normed_two, w_gate)
    up_pre = product(normed_two, w_up)
    hidden = (gate_pre * jax.nn.sigmoid(gate_pre) * up_pre).astype(jnp.bfloat16)
    output = (middle + product_nt(hidden, w_down_t)).astype(jnp.bfloat16)
    state = (
        unit_one,
        scale_one,
        normed_one,
        query,
        keys,
        values,
        mixed,
        log_sum,
        attended,
        unit_two,
        scale_two,
        normed_two,
        gate_pre,
        up_pre,
        hidden,
    )
    return (output, state)


def backward(state, block_input, w_rest, cotangent, weights):
    w_qkv, w_out, w_gate, w_up, w_down_t, gain_attn, gain_ffn = weights
    (
        unit_one,
        scale_one,
        normed_one,
        query,
        keys,
        values,
        mixed,
        log_sum,
        attended,
        unit_two,
        scale_two,
        normed_two,
        gate_pre,
        up_pre,
        hidden,
    ) = state
    rows = cotangent.shape[0]
    grad_hidden = product(cotangent, w_down_t)
    sigmoid = jax.nn.sigmoid(gate_pre)
    grad_gate = (grad_hidden * up_pre * sigmoid * (1.0 + gate_pre * (1.0 - sigmoid))).astype(
        jnp.bfloat16
    )
    grad_up = (grad_hidden * gate_pre * sigmoid).astype(jnp.bfloat16)
    grad_normed_two = product_nt(grad_gate, w_gate) + product_nt(grad_up, w_up)
    back_two, gain_two_grad = norm_backward(
        grad_normed_two, unit_two, scale_two, gain_ffn.astype(jnp.float32)
    )
    grad_middle = cotangent.astype(jnp.float32) + back_two
    cosine, sine = tables()
    gains = jnp.pad(gain_two_grad[None, :], ((1, 6), (0, 0)))
    logs = jnp.broadcast_to(log_sum.reshape(HEADS, 1, LEN), (HEADS, 8, LEN))
    return (
        cotangent.T,
        hidden,
        normed_two,
        grad_gate,
        grad_up,
        w_rest,
        query.reshape(rows, D).T,
        keys.reshape(rows, KVD).T,
        values.reshape(rows, KVD).T,
        attended.T,
        normed_one,
        logs.reshape(HEADS * 8, LEN),
        grad_middle,
        block_input.T,
        scale_one.reshape(1, rows),
        gain_attn.astype(jnp.float32).reshape(D, 1),
        gains,
        cosine.T,
        sine.T,
    )


MESH = pl.DeviceIdType.MESH
LOW = 8


def place(shard_count):
    rep = lax.axis_index("rep")
    shard = lax.axis_index("shard")
    low = rep % LOW
    return rep, shard, low


def flipped(index, step):
    bit = (index // step) % 2
    return index + step - 2 * step * bit


def greet(rep, shard, reps, shard_count):
    barrier = pltpu.get_barrier_semaphore()
    met = 0
    step = 1
    while step < reps:
        pl.semaphore_signal(
            barrier, inc=1, device_id=(flipped(rep, step), shard), device_id_type=MESH
        )
        met += 1
        step *= 2
    for ahead in range(1, shard_count):
        pl.semaphore_signal(
            barrier, inc=1, device_id=(rep, (shard + ahead) % shard_count), device_id_type=MESH
        )
        met += 1
    pl.semaphore_wait(barrier, met)


def remote(source, target, sems, index, device):
    return pltpu.make_async_remote_copy(
        src_ref=source,
        dst_ref=target,
        send_sem=sems[0].at[index],
        recv_sem=sems[1].at[index],
        device_id=device,
        device_id_type=MESH,
    )


def steps_of(half):
    return (4, 2) if half == 0 else (2, 4)


def gather_kernel(
    shard_count, own, gains, down, gate, up, rest, all_gains, buf, zs, zr, ps, pr, gs, gr, outs
):
    rep, shard, low = place(shard_count)
    greet(rep, shard, LOW, shard_count)
    finals = (down, gate, up, rest)
    rows, cols = own.shape[2:]

    def put(source, owner, chunk, half, index):
        final = finals[chunk // 2]
        lane = 2 * (chunk % 2) + half
        if chunk // 2 == 0:
            where = final.at[
                pl.ds(lane * rows, rows), pl.ds(pl.multiple_of(owner * cols, 128), cols)
            ]
        else:
            where = final.at[
                pl.ds(pl.multiple_of(owner * rows, 16), rows), pl.ds(lane * cols, cols)
            ]
        copy = pltpu.make_async_copy(source, where, outs.at[index])
        copy.start()
        return copy

    sent = []
    landed = {}
    copies = []
    for ahead in range(1, shard_count):
        device = (rep, (shard + ahead) % shard_count)
        for half in range(2):
            copy = remote(
                own.at[low, half],
                buf.at[shard, low, half],
                (zs, zr),
                2 * ahead + half,
                device,
            )
            copy.start()
            landed[ahead, half] = copy
    gain_copies = []
    for ahead in range(1, shard_count):
        device = (rep, (shard + ahead) % shard_count)
        copy = remote(gains, all_gains.at[shard], (gs, gr), ahead, device)
        copy.start()
        gain_copies.append(copy)
    all_gains[shard] = gains[...]
    for chunk in range(LOW):
        for half in range(2):
            copies.append(put(own.at[chunk, half], shard, chunk, half, 2 * chunk + half))

    pieces = [(ahead, half) for ahead in range(1, shard_count) for half in range(2)]
    base = {piece: 7 * number for number, piece in enumerate(pieces)}
    core = flipped(rep, 1)
    jobs = {}

    def pass_on(piece, slot, chunk, partner):
        ahead, half = piece
        owner = (shard + shard_count - ahead) % shard_count
        copy = remote(
            buf.at[owner, chunk, half],
            buf.at[owner, chunk, half],
            (ps, pr),
            base[piece] + slot,
            (partner, shard),
        )
        copy.start()
        jobs[piece, slot] = copy

    for piece in pieces:
        first, second = steps_of(piece[1])
        landed[piece].wait_recv()
        pass_on(piece, 0, low, flipped(rep, first))
        pass_on(piece, 1, low, flipped(rep, second))
        pass_on(piece, 3, low, core)
    for piece in pieces:
        first, second = steps_of(piece[1])
        jobs[piece, 0].wait_recv()
        pass_on(piece, 2, flipped(low, first), flipped(rep, second))
        pass_on(piece, 4, flipped(low, first), core)
    for piece in pieces:
        first, second = steps_of(piece[1])
        jobs[piece, 1].wait_recv()
        pass_on(piece, 5, flipped(low, second), core)
        jobs[piece, 2].wait_recv()
        pass_on(piece, 6, flipped(flipped(low, first), second), core)
    for number, piece in enumerate(pieces):
        ahead, half = piece
        owner = (shard + shard_count - ahead) % shard_count
        for slot in range(3, 7):
            jobs[piece, slot].wait_recv()
        for chunk in range(LOW):
            index = 2 * LOW + LOW * number + chunk
            copies.append(put(buf.at[owner, chunk, half], owner, chunk, half, index))
    for copy in landed.values():
        copy.wait_send()
    for copy in jobs.values():
        copy.wait_send()
    for copy in gain_copies:
        copy.wait()
    for copy in copies:
        copy.wait()


def pack(mats):
    down_t = mats[0]
    rows, cols = down_t.shape[0] // 4, down_t.shape[1]
    parts = [down_t.reshape(4, rows, cols)]
    for mat in mats[1:]:
        parts.append(jnp.stack([mat[:, i * cols : (i + 1) * cols] for i in range(4)]))
    return jnp.stack(parts).reshape(LOW, 2, rows, cols)


def gain_tile(first, second):
    flat = jnp.concatenate([first, second], axis=-1).astype(jnp.float32)
    pad = [(0, 0)] * (flat.ndim - 1) + [(0, 8 * 128 - flat.shape[-1])]
    return jnp.pad(flat, pad).reshape(flat.shape[:-1] + (8, 128))


def gather(own, gains, shard_count):
    rows, cols = own.shape[2:]
    full = jax.ShapeDtypeStruct((shard_count * rows, 4 * cols), jnp.bfloat16)
    full_down = jax.ShapeDtypeStruct((4 * rows, shard_count * cols), jnp.bfloat16)
    moves = 2 * shard_count
    hops = 14 * (shard_count - 1)
    dma = pltpu.SemaphoreType.DMA
    return pl.pallas_call(
        lambda *refs: gather_kernel(shard_count, *refs),
        name="gather_weights",
        out_shape=(
            full_down,
            full,
            full,
            full,
            jax.ShapeDtypeStruct((shard_count, 8, 128), jnp.float32),
        ),
        in_specs=[pl.BlockSpec(memory_space=pltpu.VMEM)] * 2,
        out_specs=tuple(
            [pl.BlockSpec(memory_space=pl.ANY)] * 4 + [pl.BlockSpec(memory_space=pltpu.VMEM)]
        ),
        scratch_shapes=[
            pltpu.VMEM((shard_count, LOW, 2, rows, cols), jnp.bfloat16),
            dma((moves,)),
            dma((moves,)),
            dma((hops,)),
            dma((hops,)),
            dma((shard_count,)),
            dma((shard_count,)),
            dma((2 * LOW * shard_count,)),
        ],
        compiler_params=pltpu.CompilerParams(collective_id=0, has_side_effects=True),
    )(own, gains)


def add_low(left, right):
    return (left.astype(jnp.float32) + right.astype(jnp.float32)).astype(jnp.bfloat16)


def nt(left, right):
    return product_nt(left, right)


def attend_group(group, q_t, k_t, v_t, a_t, ga_t, lse, cos_t, sin_t, dqkv_t, dk_acc, dv_acc):
    here = pl.ds(group * HEAD_DIM, HEAD_DIM)
    keys, values = k_t[here, :], v_t[here, :]
    half_dim = HEAD_DIM // 2
    scale = 1.0 / math.sqrt(HEAD_DIM)
    row_ids = lax.broadcasted_iota(jnp.int32, (LEN, LEN), 0)
    col_ids = lax.broadcasted_iota(jnp.int32, (LEN, LEN), 1)

    def turn_back(grads):
        scaled = grads * sin_t[...]
        turned = jnp.concatenate([scaled[half_dim:], -scaled[:half_dim]], axis=0)
        return (grads * cos_t[...] + turned).astype(jnp.bfloat16)

    dk_acc[...] = jnp.zeros_like(dk_acc)
    dv_acc[...] = jnp.zeros_like(dv_acc)
    each = HEADS // KV_HEADS

    def head(number, carry):
        index = group * each + number
        rows = pl.ds(pl.multiple_of(index * HEAD_DIM, HEAD_DIM), HEAD_DIM)
        query, grad = q_t[rows, :], ga_t[rows, :]
        delta = jnp.sum(
            grad.astype(jnp.float32) * a_t[rows, :].astype(jnp.float32), axis=0, keepdims=True
        )
        scores = product_tn(keys, query) * scale
        scores = jnp.where(row_ids <= col_ids, scores, -1e30)
        probs = jnp.exp(scores - lse[pl.ds(pl.multiple_of(index * 8, 8), 1), :])
        dv_acc[...] += nt(grad, probs.astype(jnp.bfloat16))
        grad_scores = (probs * (product_tn(values, grad) - delta) * scale).astype(jnp.bfloat16)
        dqkv_t[rows, :] = turn_back(product(keys, grad_scores))
        dk_acc[...] += nt(query, grad_scores)
        return carry

    lax.fori_loop(0, each, head, 0)
    dqkv_t[pl.ds(D + group * HEAD_DIM, HEAD_DIM), :] = turn_back(dk_acc[...])
    dqkv_t[pl.ds(D + KVD + group * HEAD_DIM, HEAD_DIM), :] = dv_acc[...].astype(jnp.bfloat16)


def reduce_kernel(
    reps,
    shard_count,
    cot_t,
    hidden,
    normed,
    grad_gate,
    grad_up,
    rest,
    q_t,
    k_t,
    v_t,
    a_t,
    normed_one,
    lse,
    grad_middle,
    x_t,
    scale_one,
    gain_one,
    gains,
    cos_t,
    sin_t,
    total,
    gain_total,
    grad_in_t,
    grads,
    core_in,
    one_in,
    two_in,
    shard_in,
    late_out,
    late_in,
    gain_work,
    gain_in,
    gain_shard_in,
    ga_t,
    dqkv_t,
    dk_acc,
    dv_acc,
    cs,
    cr,
    os,
    orr,
    ts,
    tr,
    zs,
    zr,
    ls,
    lr,
    ps,
    pr,
    gs,
    gr,
):
    rep, shard, low = place(shard_count)
    greet(rep, shard, reps, shard_count)
    rows, cols = total.shape[3:]
    core = flipped(rep, 1)
    mine, mid, high = low % 2, (low // 2) % 2, low // 4
    lane_mine = low // 2
    order = list(range(1, shard_count)) + [0]
    copies = []

    def owner_of(ahead):
        return (shard + ahead) % shard_count

    def launch(source, target, sems, index, device):
        copy = remote(source, target, sems, index, device)
        copy.start()
        copies.append(copy)
        return copy

    swaps, ones, twos, lands, jobs = {}, {}, {}, {}, {}

    def swap(matrix):
        for ahead in order:
            swaps[matrix, ahead] = launch(
                grads.at[owner_of(ahead), matrix, 1 - mine],
                core_in.at[matrix, ahead],
                (cs, cr),
                matrix * shard_count + ahead,
                (core, shard),
            )

    def fill(matrix, lane, value):
        for owner in range(shard_count):
            for part in range(2):
                start = (2 * owner + part) * rows
                grads[owner, matrix, part, lane] = value[start : start + rows].astype(jnp.bfloat16)

    def stage_one(matrix, ahead):
        owner = owner_of(ahead)
        swaps[matrix, ahead].wait_recv()
        for lane in range(4):
            grads[owner, matrix, mine, lane] = add_low(
                grads[owner, matrix, mine, lane], core_in[matrix, ahead, lane]
            )
        for other in range(2):
            lane = 2 * (1 - high) + other if matrix % 2 == 0 else 2 * other + 1 - mid
            ones[matrix, ahead, other] = launch(
                grads.at[owner, matrix, mine, lane],
                one_in.at[matrix, ahead, other],
                (os, orr),
                (matrix * shard_count + ahead) * 2 + other,
                (flipped(rep, steps_of(matrix % 2)[0]), shard),
            )

    def stage_two(matrix, ahead):
        owner = owner_of(ahead)
        for other in range(2):
            ones[matrix, ahead, other].wait_recv()
            lane = 2 * high + other if matrix % 2 == 0 else 2 * other + mid
            grads[owner, matrix, mine, lane] = add_low(
                grads[owner, matrix, mine, lane], one_in[matrix, ahead, other]
            )
        lane = 2 * high + 1 - mid if matrix % 2 == 0 else 2 * (1 - high) + mid
        twos[matrix, ahead] = launch(
            grads.at[owner, matrix, mine, lane],
            two_in.at[matrix, ahead],
            (ts, tr),
            matrix * shard_count + ahead,
            (flipped(rep, steps_of(matrix % 2)[1]), shard),
        )

    def stage_three(matrix, ahead):
        owner = owner_of(ahead)
        twos[matrix, ahead].wait_recv()
        grads[owner, matrix, mine, lane_mine] = add_low(
            grads[owner, matrix, mine, lane_mine], two_in[matrix, ahead]
        )
        if ahead:
            lands[matrix, ahead] = launch(
                grads.at[owner, matrix, mine, lane_mine],
                shard_in.at[matrix, ahead],
                (zs, zr),
                matrix * shard_count + ahead,
                (rep, owner),
            )

    def pass_on(matrix, slot, part, lane, partner):
        jobs[matrix, slot] = launch(
            total.at[matrix, part, lane],
            total.at[matrix, part, lane],
            (ps, pr),
            7 * matrix + slot,
            (partner, shard),
        )

    def finish(matrix):
        running = grads[shard, matrix, mine, lane_mine].astype(jnp.float32)
        for ahead in range(1, shard_count):
            lands[matrix, ahead].wait_recv()
            running = running + shard_in[matrix, ahead].astype(jnp.float32)
        step, number = LOW, 0
        while step < reps:
            late_out[number, matrix] = running.astype(jnp.bfloat16)
            copy = launch(
                late_out.at[number, matrix],
                late_in.at[number, matrix],
                (ls, lr),
                4 * number + matrix,
                (flipped(rep, step), shard),
            )
            copy.wait_recv()
            running = late_out[number, matrix].astype(jnp.float32) + late_in[
                number, matrix
            ].astype(jnp.float32)
            step, number = 2 * step, number + 1
        total[matrix, mine, lane_mine] = running.astype(jnp.bfloat16)
        first, second = steps_of(matrix % 2)
        pass_on(matrix, 0, mine, lane_mine, flipped(rep, first))
        pass_on(matrix, 1, mine, lane_mine, flipped(rep, second))
        pass_on(matrix, 3, mine, lane_mine, core)

    def spread_one(matrix):
        first, second = steps_of(matrix % 2)
        jobs[matrix, 0].wait_recv()
        pass_on(matrix, 2, mine, flipped(low, first) // 2, flipped(rep, second))
        pass_on(matrix, 4, mine, flipped(low, first) // 2, core)

    def spread_two(matrix):
        first, second = steps_of(matrix % 2)
        jobs[matrix, 1].wait_recv()
        pass_on(matrix, 5, mine, flipped(low, second) // 2, core)
        jobs[matrix, 2].wait_recv()
        pass_on(matrix, 6, mine, flipped(flipped(low, first), second) // 2, core)

    def tasks_of(matrices):
        listed = []
        for place_of, matrix in enumerate(matrices):
            for number, ahead in enumerate(order):
                spot = 4 * place_of + number
                for turn, stage in enumerate((stage_one, stage_two, stage_three)):
                    listed.append((spot + 4 * turn, turn, stage, (matrix, ahead)))
            last = 4 * place_of + 3 + 8
            for turn, stage in enumerate((finish, spread_one, spread_two)):
                listed.append((last + 5 + 2 * turn, 3 + turn, stage, (matrix,)))
        listed.sort(key=lambda item: item[:2])
        return listed

    def run(listed):
        for item in listed:
            item[2](*item[3])

    for owner in range(shard_count):
        value = product(cot_t[...], hidden[:, owner * cols : (owner + 1) * cols])
        for lane in range(4):
            for part in range(2):
                start = (2 * lane + part) * rows
                grads[owner, 0, part, lane] = value[start : start + rows].astype(jnp.bfloat16)
    swap(0)
    turned = normed[...].T
    for matrix, source in ((1, grad_gate), (2, grad_up)):
        for lane in range(4):
            fill(matrix, lane, product(turned, source[:, lane * cols : (lane + 1) * cols]))
        swap(matrix)
    waiting = tasks_of((0, 1, 2))
    run(waiting[:10])
    middle_low = grad_middle[...].astype(jnp.bfloat16)
    width = D + 2 * KVD
    ga_t[...] = nt(rest[:, width:], middle_low).astype(jnp.bfloat16)
    out_grad = product(a_t[...], middle_low)
    run(waiting[10:14])
    cuts = [14, 23, 32, len(waiting)]
    for group in range(KV_HEADS):
        attend_group(
            group, q_t, k_t, v_t, a_t, ga_t, lse, cos_t, sin_t, dqkv_t, dk_acc, dv_acc
        )
        if group < KV_HEADS - 1:
            run(waiting[cuts[group] : cuts[group + 1]])
    turned = normed_one[...].T
    for lane in range(2):
        fill(3, lane, nt(turned, dqkv_t[lane * cols : (lane + 1) * cols, :]))
    mixed = jnp.concatenate([nt(turned, dqkv_t[2 * cols :, :]), out_grad], axis=1)
    for lane in range(2):
        fill(3, 2 + lane, mixed[:, lane * cols : (lane + 1) * cols])
    swap(3)
    run(waiting[cuts[2] :])
    last = tasks_of((3,))
    run(last[:4])

    back = product(rest[:, :width], dqkv_t[...])
    unit = x_t[...].astype(jnp.float32) * scale_one[...]
    spread = back * unit
    inner = back * gain_one[...]
    mean = jnp.sum(inner * unit, axis=0, keepdims=True) * (1.0 / D)
    grad_in_t[...] = (
        grad_middle[...].T + scale_one[...] * (inner - unit * mean)
    ).astype(jnp.bfloat16)
    column = jnp.sum(spread, axis=1, keepdims=True)
    gain_work[0] = gains[...]
    gain_work[0, 0:1] = jnp.broadcast_to(column, (D, 128)).T[0:1]

    pending = last[4:]
    step, number = 1, 0
    while step < reps:
        copy = launch(
            gain_work.at[number], gain_in.at[number], (gs, gr), number, (flipped(rep, step), shard)
        )
        run(pending[:2])
        pending = pending[2:]
        copy.wait_recv()
        gain_work[number + 1] = gain_work[number] + gain_in[number]
        step, number = 2 * step, number + 1
    gain_shards = {}
    for ahead in range(1, shard_count):
        gain_shards[ahead] = launch(
            gain_work.at[number],
            gain_shard_in.at[ahead],
            (gs, gr),
            number + ahead,
            (rep, owner_of(ahead)),
        )
    run(pending)
    running = gain_work[number]
    for ahead in range(1, shard_count):
        gain_shards[ahead].wait_recv()
        running = running + gain_shard_in[ahead]
    gain_total[...] = running
    for matrix in range(4):
        for slot in range(3, 7):
            jobs[matrix, slot].wait_recv()
    for copy in copies:
        copy.wait_send()


def reduce_all(operands, reps, shard_count):
    rows, cols = D // 8, D * 2 // 3
    dma = pltpu.SemaphoreType.DMA
    low = jnp.bfloat16
    bits = reps.bit_length() - 1
    late = max(bits - 3, 1)
    sems = []
    for count in (
        4 * shard_count,
        8 * shard_count,
        4 * shard_count,
        4 * shard_count,
        4 * late,
        28,
        bits + shard_count,
    ):
        sems += [dma((count,)), dma((count,))]
    return pl.pallas_call(
        lambda *refs: reduce_kernel(reps, shard_count, *refs),
        name="reduce_grads",
        out_shape=(
            jax.ShapeDtypeStruct((4, 2, 4, rows, cols), low),
            jax.ShapeDtypeStruct((8, D), jnp.float32),
            jax.ShapeDtypeStruct((D, LEN), low),
        ),
        in_specs=[pl.BlockSpec(memory_space=pltpu.VMEM)] * len(operands),
        out_specs=tuple([pl.BlockSpec(memory_space=pltpu.VMEM)] * 3),
        scratch_shapes=[
            pltpu.VMEM((shard_count, 4, 2, 4, rows, cols), low),
            pltpu.VMEM((4, shard_count, 4, rows, cols), low),
            pltpu.VMEM((4, shard_count, 2, rows, cols), low),
            pltpu.VMEM((4, shard_count, rows, cols), low),
            pltpu.VMEM((4, shard_count, rows, cols), low),
            pltpu.VMEM((late, 4, rows, cols), low),
            pltpu.VMEM((late, 4, rows, cols), low),
            pltpu.VMEM((bits + 1, 8, D), jnp.float32),
            pltpu.VMEM((bits, 8, D), jnp.float32),
            pltpu.VMEM((shard_count, 8, D), jnp.float32),
            pltpu.VMEM((D, LEN), low),
            pltpu.VMEM((D + 2 * KVD, LEN), low),
            pltpu.VMEM((HEAD_DIM, LEN), jnp.float32),
            pltpu.VMEM((HEAD_DIM, LEN), jnp.float32),
        ]
        + sems,
        compiler_params=pltpu.CompilerParams(
            collective_id=1, has_side_effects=True, vmem_limit_bytes=60000 * 1024
        ),
    )(*operands)


def shards(
    reps,
    shard_count,
    block_input,
    w_query,
    w_key,
    w_value,
    w_out,
    w_gate,
    w_up,
    w_down,
    gain_attn,
    gain_ffn,
    cotangent,
):
    rest = jnp.concatenate([w_query, w_key, w_value, w_out], axis=1)
    own = pack((w_down.T, w_gate, w_up, rest))
    full_down_t, full_gate, full_up, full_rest, tiles = gather(
        own, gain_tile(gain_attn, gain_ffn), shard_count
    )
    each = D // shard_count
    flat = tiles.reshape(shard_count, -1)
    full_gain_attn = flat[:, :each].reshape(-1)
    full_gain_ffn = flat[:, each : 2 * each].reshape(-1)
    width = D + 2 * KVD
    weights = (
        full_rest[:, :width],
        full_rest[:, width:],
        full_gate,
        full_up,
        full_down_t,
        full_gain_attn,
        full_gain_ffn,
    )
    output, state = forward(block_input, weights)
    operands = backward(state, block_input, full_rest, cotangent, weights)
    total, gain_total, grad_in_t = reduce_all(operands, reps, shard_count)
    grad_input = grad_in_t.T
    rows, cols = total.shape[3:]
    blocks = total.astype(jnp.float32)

    def wide(matrix):
        return blocks[matrix].transpose(0, 2, 1, 3).reshape(2 * rows, 4 * cols)

    grad_rest = wide(3)
    own_gains = lax.dynamic_slice(
        gain_total, (0, lax.axis_index("shard") * each), (2, each)
    )
    return (
        output,
        grad_input,
        grad_rest[:, :D],
        grad_rest[:, D : D + KVD],
        grad_rest[:, D + KVD : width],
        grad_rest[:, width:],
        wide(1),
        wide(2),
        blocks[0].transpose(1, 0, 2, 3).reshape(8 * rows, cols).T,
        own_gains[0],
        own_gains[1],
    )


def solution(mesh):
    placed = (
        P(("rep", "shard"), None),
        P("shard", None),
        P("shard", None),
        P("shard", None),
        P("shard", None),
        P("shard", None),
        P("shard", None),
        P("shard", None),
        P("shard"),
        P("shard"),
        P(("rep", "shard"), None),
    )
    return jax.shard_map(
        lambda *args: shards(mesh.shape["rep"], mesh.shape["shard"], *args),
        mesh=mesh,
        in_specs=placed,
        out_specs=(
            P(("rep", "shard"), None),
            P(("rep", "shard"), None),
            P("shard", None),
            P("shard", None),
            P("shard", None),
            P("shard", None),
            P("shard", None),
            P("shard", None),
            P("shard", None),
            P("shard"),
            P("shard"),
        ),
        check_vma=False,
    )
```
